32 devices in a mesh: dp: 8 (over z, core), fsdp: 4 (over y, x).
Axes of the slice: x: 2, y: 2, z: 4, core: 2. Of those that a mesh axis runs over, the one named last changes fastest.
Arguments:
- inputs: bfloat16 [64, 512, 768], P(('dp', 'fsdp')), may hold values from -6 to 6
- segment_ids: int32 [64, 512], P(('dp', 'fsdp')), may hold values from 0 to 3, never falling along the last dimension, each value on 1 to 256 neighbouring positions
- cotangent: bfloat16 [64, 512, 768], P(('dp', 'fsdp')), may hold values from -9 to 9
- qkv_weight: bfloat16 [768, 2304], P(('dp', 'fsdp')), may hold values from -0.21875 to 0.21875
- out_weight: bfloat16 [768, 768], P(('dp', 'fsdp')), may hold values from -1.75 to 1.75
- up_weight: bfloat16 [768, 3072], P(('dp', 'fsdp')), may hold values from -0.21875 to 0.21875
- down_weight: bfloat16 [3072, 768], P(('dp', 'fsdp')), may hold values from -0.109375 to 0.109375
- query_bias_vector: bfloat16 [768], P(('dp', 'fsdp')), may hold values from -1.5 to 1.5
- value_bias_vector: bfloat16 [768], P(('dp', 'fsdp')), may hold values from -1.5 to 1.5
- out_bias: bfloat16 [768], P(('dp', 'fsdp')), may hold values from -1.5 to 1.5
- gain_one: bfloat16 [768], P(('dp', 'fsdp')), may hold values from 0.5 to 1.5
- shift_one: bfloat16 [768], P(('dp', 'fsdp')), may hold values from -1.5 to 1.5
- up_bias: bfloat16 [3072], P(('dp', 'fsdp')), may hold values from -1.5 to 1.5
- down_bias: bfloat16 [768], P(('dp', 'fsdp')), may hold values from -1.5 to 1.5
- gain_two: bfloat16 [768], P(('dp', 'fsdp')), may hold values from 0.5 to 1.5
- shift_two: bfloat16 [768], P(('dp', 'fsdp')), may hold values from -1.5 to 1.5
- query_down: bfloat16 [768, 8], replicated, may hold values from -0.21875 to 0.21875
- query_up_weight: bfloat16 [8, 768], replicated, may hold values from -2 to 2
- value_down: bfloat16 [768, 8], replicated, may hold values from -0.21875 to 0.21875
- value_up_weight: bfloat16 [8, 768], replicated, may hold values from -2 to 2
Outputs:
- output: bfloat16 [64, 512, 768], P(('dp', 'fsdp'))
- grad_input: float32 [64, 512, 768], P(('dp', 'fsdp'))
- grad_query_down: float32 [768, 8], replicated
- grad_query_up: float32 [8, 768], replicated
- grad_value_down: float32 [768, 8], replicated
- grad_value_up: float32 [8, 768], replicated
The draws below stay inside these ranges and needn't reach their ends.
Inputs may be any that keep to these rules, and one draw needn't show every extreme that they name: `segment_ids`: within a pack the ids never fall; each of the 4 documents has 1 to 256 rows, and one has exactly 256.
All inputs are finite; a program needn't handle non-finite values.
Results may differ from the reference program's by a relative error of at most 0.015.
The reference program's roundings to bfloat16 on the way count: a program that leaves them out, or rounds other values in their place, can miss the bound.
Values may be sent and summed in bfloat16 or wider, within the bound.
No kernel may reach another device: no remote copies, remote signals or barrier semaphores. Data moves between devices by JAX's collectives and lax.ppermute only.
A program may use at most 128 MiB of HBM per device.

```python
import math
import jax
import jax.numpy as jnp
import numpy as np
from jax import lax

MODEL_WIDTH = 768
HEADS = 12
HEAD_DIM = 64
FF = 3072
RANK = 8
SEQ = 512
SEGS = 4
PACKS = 64


def draw_cotangent(key, part):
    pack_scale = 0.6 + 1.2 * jnp.arange(PACKS, dtype=jnp.float32) / max(PACKS - 1, 1)
    base = jnp.clip(jax.random.normal(key, (PACKS, SEQ, MODEL_WIDTH), jnp.float32), -5.0, 5.0)
    return (base * pack_scale[:, None, None]).astype(jnp.bfloat16)


def levels(stream_key, dims, pieces, low, largest):
    factor_of = 1.0
    for dim, shards_of in pieces:
        draws = jax.random.uniform(jax.random.fold_in(jax.random.fold_in(stream_key, 6), dim), (shards_of,), jnp.float32, low / len(pieces), largest / len(pieces))
        factor_of = factor_of * jnp.repeat(jnp.exp(draws), dims[dim] // shards_of).reshape((-1,) + (1,) * (len(dims) - 1 - dim))
    return factor_of


def split_up(number_of, total, most, slope):
    loads = [(1 << 20) // math.isqrt(standing ** slope) + 1 for standing in range(2, number_of + 1)]
    surplus, given = total - most - (number_of - 1), [1] * (number_of - 1)
    while surplus > 0:
        movable = [i for i in range(number_of - 1) if given[i] < most]
        whole, remaining = sum([loads[i] for i in movable]), surplus
        for i in movable:
            more = min(most - given[i], max(1, remaining * loads[i] // whole), surplus)
            given[i] = given[i] + more
            surplus = surplus - more
    return np.array([most] + given)


def uneven(stream_key, amount, total, limit, skew):
    if amount == 2:
        one = jax.random.randint(stream_key, (), max(1, total - limit), min(limit, total - 1) + 1)
        return jnp.stack([one, total - one])
    sizes = jnp.asarray(split_up(amount, total, limit, skew), jnp.int32)
    twos = (amount - 1) // 2
    giver, taker = sizes[1:1 + 2 * twos:2], sizes[2:2 + 2 * twos:2]
    margin = jnp.minimum(giver - 1, limit - taker)
    shifted = jax.random.randint(jax.random.fold_in(stream_key, 1), (twos,), 0, 1 << 20) % (margin + 1)
    sizes = sizes.at[1:1 + 2 * twos:2].set(giver - shifted).at[2:2 + 2 * twos:2].set(taker + shifted)
    return sizes[jax.random.permutation(jax.random.fold_in(stream_key, 2), amount)]


def normal_values(stream_key, shape, deviation, limit, shards=(), held_as=jnp.bfloat16):
    loudness = levels(stream_key, shape, shards, -0.22, 0.18) if shards else 1.0
    drawn = jax.random.normal(stream_key, shape, jnp.float32) * deviation * loudness
    return jnp.minimum(jnp.maximum(drawn, -limit), limit).astype(held_as)


def setup_inputs(seed: int = 0) -> dict:
    splits = jax.random.split(jax.random.key(seed), 21)
    inputs = normal_values(splits[0], (PACKS, SEQ, MODEL_WIDTH), 1.0, 6.0, ((0, 32),))
    segment_ids = jax.vmap(lambda own: jnp.searchsorted(jnp.cumsum(uneven(own, SEGS, SEQ, SEQ // 2, 2)), jnp.arange(SEQ), side="right"))(jax.random.split(splits[1], PACKS)).reshape((PACKS, SEQ)).astype(jnp.int32)
    cotangent = draw_cotangent(jax.random.fold_in(splits[20], 71), 0)
    qkv_weight = normal_values(splits[3], (MODEL_WIDTH, 3 * MODEL_WIDTH), MODEL_WIDTH ** -0.5, 0.21875, ((0, 32),))
    out_weight = normal_values(splits[4], (MODEL_WIDTH, MODEL_WIDTH), (MODEL_WIDTH // 64) ** -0.5, 1.75, ((0, 32),))
    up_weight = normal_values(splits[5], (MODEL_WIDTH, FF), MODEL_WIDTH ** -0.5, 0.21875, ((0, 32),))
    down_weight = normal_values(splits[6], (FF, MODEL_WIDTH), FF ** -0.5, 0.109375, ((0, 32),))
    query_bias_vector = normal_values(splits[7], (MODEL_WIDTH,), 0.3, 1.5, ((0, 32),))
    value_bias_vector = normal_values(splits[8], (MODEL_WIDTH,), 0.3, 1.5, ((0, 32),))
    out_bias = normal_values(splits[9], (MODEL_WIDTH,), 0.3, 1.5, ((0, 32),))
    gain_one = jnp.clip(1.0 + 0.1 * jax.random.normal(splits[10], (MODEL_WIDTH,), jnp.float32), 0.5, 1.5).astype(jnp.bfloat16)
    shift_one = normal_values(splits[11], (MODEL_WIDTH,), 0.3, 1.5, ((0, 32),))
    up_bias = normal_values(splits[12], (FF,), 0.3, 1.5, ((0, 32),))
    down_bias = normal_values(splits[13], (MODEL_WIDTH,), 0.3, 1.5, ((0, 32),))
    gain_two = jnp.clip(1.0 + 0.1 * jax.random.normal(splits[14], (MODEL_WIDTH,), jnp.float32), 0.5, 1.5).astype(jnp.bfloat16)
    shift_two = normal_values(splits[15], (MODEL_WIDTH,), 0.3, 1.5, ((0, 32),))
    query_down = normal_values(splits[16], (MODEL_WIDTH, RANK), MODEL_WIDTH ** -0.5, 0.21875)
    query_up_weight = normal_values(splits[17], (RANK, MODEL_WIDTH), RANK ** -0.5, 2.0)
    value_down = normal_values(splits[18], (MODEL_WIDTH, RANK), MODEL_WIDTH ** -0.5, 0.21875)
    value_up_weight = normal_values(splits[19], (RANK, MODEL_WIDTH), RANK ** -0.5, 2.0)
    return dict(inputs=inputs, segment_ids=segment_ids, cotangent=cotangent, qkv_weight=qkv_weight, out_weight=out_weight, up_weight=up_weight, down_weight=down_weight, query_bias_vector=query_bias_vector, value_bias_vector=value_bias_vector, out_bias=out_bias, gain_one=gain_one, shift_one=shift_one, up_bias=up_bias, down_bias=down_bias, gain_two=gain_two, shift_two=shift_two, query_down=query_down, query_up_weight=query_up_weight, value_down=value_down, value_up_weight=value_up_weight)


highest_precision_mode = lax.Precision.HIGHEST
norm_epsilon = 1e-05
adapter_scale = 2.0

@jax.custom_vjp
def rank_rows(v):
    return lax.optimization_barrier(v.astype(jnp.bfloat16)).astype(jnp.float32)

@jax.custom_vjp
def rank_rows_gradient(v):
    return v

def low_keep(v):
    return (rank_rows(v), None)

def low_pass(kept, grad):
    return (grad,)

def back_keep(v):
    return (v, None)

def back_low(kept, grad):
    return (rank_rows(grad),)
rank_rows.defvjp(low_keep, low_pass)
rank_rows_gradient.defvjp(back_keep, back_low)

def matrix_multiply(left, right):
    return jnp.dot(left, right, precision=highest_precision_mode, preferred_element_type=jnp.float32)

def layer_norm(value_rows, gain, shift):
    centred = value_rows - lax.optimization_barrier(jnp.mean(value_rows, axis=-1, keepdims=True))
    variance = lax.optimization_barrier(jnp.mean(centred * centred, axis=-1, keepdims=True))
    return centred * lax.rsqrt(variance + norm_epsilon) * gain + shift

def layer_forward(rows_in, segment, frozen, adapters):
    qkv_weight, out_weight, up_weight, down_weight, query_bias_vector, value_bias_vector, out_bias, gain_one, shift_one, up_bias, down_bias, gain_two, shift_two = frozen
    query_down, query_up_weight, value_down, value_up_weight = adapters
    rounded_input = rank_rows(rows_in)
    projected_rows = matrix_multiply(rounded_input, qkv_weight)
    query_rank_rows = matrix_multiply(rounded_input, query_down)
    value_rank_rows = matrix_multiply(rounded_input, value_down)
    query_rows = rank_rows(rank_rows_gradient(projected_rows[:, :MODEL_WIDTH] + query_bias_vector + adapter_scale * matrix_multiply(query_rank_rows, query_up_weight)))
    key_rows = rank_rows(rank_rows_gradient(projected_rows[:, MODEL_WIDTH:2 * MODEL_WIDTH]))
    value_rows = rank_rows(rank_rows_gradient(projected_rows[:, 2 * MODEL_WIDTH:] + value_bias_vector + adapter_scale * matrix_multiply(value_rank_rows, value_up_weight)))
    query_rows = query_rows.reshape(SEQ, HEADS, HEAD_DIM)
    key_rows = key_rows.reshape(SEQ, HEADS, HEAD_DIM)
    value_rows = value_rows.reshape(SEQ, HEADS, HEAD_DIM)
    raw_scores = rank_rows_gradient(jnp.einsum('qhd,khd->hqk', query_rows, key_rows, precision=highest_precision_mode))
    scores = raw_scores * HEAD_DIM ** (-0.5)
    in_segment = (segment[:, None] == segment[None, :])[None]
    masked = jnp.where(in_segment, scores, -jnp.inf)
    highest = lax.optimization_barrier(jnp.max(masked, axis=-1, keepdims=True))
    exponent = jnp.where(in_segment, jnp.exp(masked - highest), 0.0)
    probs = exponent / lax.optimization_barrier(jnp.sum(exponent, axis=-1, keepdims=True))
    mixed = jnp.einsum('hqk,khd->qhd', rank_rows(probs), value_rows, precision=highest_precision_mode)
    attended = rank_rows(rank_rows_gradient(mixed.reshape(SEQ, MODEL_WIDTH)))
    branch = rank_rows_gradient(matrix_multiply(attended, out_weight) + out_bias)
    normed_one = layer_norm(rows_in + branch, gain_one, shift_one)
    upper = rank_rows_gradient(matrix_multiply(rank_rows(normed_one), up_weight) + up_bias)
    activated = rank_rows(jax.nn.gelu(upper, approximate=False))
    ffn_out = rank_rows_gradient(matrix_multiply(activated, down_weight) + down_bias)
    return layer_norm(normed_one + ffn_out, gain_two, shift_two)

def reference(inputs, segment_ids, cotangent, qkv_weight, out_weight, up_weight, down_weight, query_bias_vector, value_bias_vector, out_bias, gain_one, shift_one, up_bias, down_bias, gain_two, shift_two, query_down, query_up_weight, value_down, value_up_weight):
    frozen = tuple((weight.astype(jnp.float32) for weight in (qkv_weight, out_weight, up_weight, down_weight, query_bias_vector, value_bias_vector, out_bias, gain_one, shift_one, up_bias, down_bias, gain_two, shift_two)))
    adapters = tuple((weight.astype(jnp.float32) for weight in (query_down, query_up_weight, value_down, value_up_weight)))

    def advance(summed, packed):
        pack_rows, pack_segments, pack_cotangent = packed

        def forward(rows_in, adapter_set):
            return layer_forward(rows_in, pack_segments, frozen, adapter_set)
        result, pullback = jax.vjp(forward, pack_rows.astype(jnp.float32), adapters)
        grad_rows, grad_adapters = pullback(pack_cotangent.astype(jnp.float32))
        summed = jax.tree.map(lambda first, second: first + second, summed, grad_adapters)
        return (summed, (result.astype(jnp.bfloat16), grad_rows))
    initial = tuple((jnp.zeros(weight.shape, jnp.float32) for weight in adapters))
    summed, (outputs, grad_rows) = lax.scan(advance, initial, (inputs, segment_ids, cotangent))
    return (outputs, grad_rows, summed[0], summed[1], summed[2], summed[3])
```

```python
from functools import partial

import jax
import jax.numpy as jnp
from jax import lax
from jax.experimental import pallas as pl
from jax.experimental.pallas import tpu as pltpu
from jax.sharding import PartitionSpec as P

HEADS = 12
HEAD_DIM = 64
AXES = ("dp", "fsdp")


highest_precision_mode = lax.Precision.HIGHEST
norm_epsilon = 1e-05
adapter_scale = 2.0


def log_two(number):
    return number.bit_length() - 1


def step_masks(dp, fsdp):
    z_count = dp // 2
    z_bits, f_bits = log_two(z_count), log_two(fsdp)
    x_bits = f_bits // 2
    z_zero = [1 << i for i in range(z_bits)]
    z_one = ([z_count - 1] + [1 << i for i in range(z_bits - 1)]) if z_bits else []
    x = [1 << i for i in range(x_bits)]
    y = [1 << i for i in range(x_bits, f_bits)]
    zero = [(m, 0) for m in z_zero] + [(0, m) for m in x + y]
    one = [(m, 0) for m in z_one] + [(0, m) for m in y + x]
    return list(zip(zero, one))


def step_pairs(dp, fsdp, steps):
    pairs = []
    for d in range(dp):
        mz, mf = steps[d % 2]
        for f in range(fsdp):
            target = ((((d // 2) ^ mz) * 2) + d % 2) * fsdp + (f ^ mf)
            pairs.append((d * fsdp + f, target))
    return pairs


def core_pairs(dp, fsdp):
    return [(d * fsdp + f, (d ^ 1) * fsdp + f) for d in range(dp) for f in range(fsdp)]


def shard_offsets(steps, core):
    masks = [(0, 0)]
    for step in steps:
        mz, mf = step[core]
        masks = masks + [(z ^ mz, f ^ mf) for z, f in masks]
    return masks


def shard_order(dp, fsdp):
    steps = step_masks(dp, fsdp)
    tables = [jnp.array(shard_offsets(steps, core), jnp.int32) for core in (0, 1)]
    d, f = lax.axis_index("dp"), lax.axis_index("fsdp")
    z, core = d // 2, d % 2
    mine = jnp.where(core == 0, tables[0], tables[1])
    other = jnp.where(core == 0, tables[1], tables[0])
    first = ((z ^ mine[:, 0]) * 2 + core) * fsdp + (f ^ mine[:, 1])
    second = ((z ^ other[:, 0]) * 2 + (1 - core)) * fsdp + (f ^ other[:, 1])
    return jnp.concatenate([first, second])


def gather(shard, dp, fsdp):
    buffer = shard[None]
    for steps in step_masks(dp, fsdp):
        got = lax.ppermute(buffer, AXES, step_pairs(dp, fsdp, steps))
        buffer = jnp.concatenate([buffer, got], axis=0)
    return buffer, lax.ppermute(buffer, AXES, core_pairs(dp, fsdp))


def assemble_kernel(order_ref, own_ref, other_ref, out_ref, sems):
    half = own_ref.shape[0]
    copies = []
    for place in range(2 * half):
        source = own_ref.at[place] if place < half else other_ref.at[place - half]
        copies.append(pltpu.make_async_copy(source, out_ref.at[order_ref[place]], sems.at[place]))
    for copy in copies:
        copy.start()
    for copy in copies:
        copy.wait()


def assemble(order, own, other):
    places = order.shape[0]
    anywhere = pl.BlockSpec(memory_space=pl.ANY)
    whole = pl.pallas_call(
        assemble_kernel,
        out_shape=jax.ShapeDtypeStruct((places,) + own.shape[1:], own.dtype),
        grid_spec=pltpu.PrefetchScalarGridSpec(
            num_scalar_prefetch=1,
            grid=(1,),
            in_specs=[anywhere, anywhere],
            out_specs=anywhere,
            scratch_shapes=[pltpu.SemaphoreType.DMA((places,))],
        ),
        name="assemble",
    )(order, own, other)
    return whole.reshape((places * own.shape[1],) + own.shape[2:])


def sum_everywhere(value, dp, fsdp):
    value = value + lax.ppermute(value, AXES, core_pairs(dp, fsdp))
    for steps in step_masks(dp, fsdp):
        value = value + lax.ppermute(value, AXES, step_pairs(dp, fsdp, (steps[0], steps[0])))
    return value


def layer_norm(value_rows, gain, shift):
    centred = value_rows - jnp.mean(value_rows, axis=-1, keepdims=True)
    variance = jnp.mean(centred * centred, axis=-1, keepdims=True)
    return centred * lax.rsqrt(variance + norm_epsilon) * gain + shift


def gelu_exact(value_rows):
    return jax.nn.gelu(value_rows, approximate=False)


def segment_mask(segment):
    return (segment[:, None] == segment[None, :])[None]


def attend_pack(packed):
    query_rows, key_rows, value_rows, segment = packed
    scale = query_rows.shape[-1] ** (-0.5)
    raw_scores = jnp.einsum(
        "qhd,khd->hqk", query_rows, key_rows, preferred_element_type=jnp.float32
    )
    in_segment = segment_mask(segment)
    masked = jnp.where(in_segment, raw_scores * scale, -jnp.inf)
    highest = jnp.max(masked, axis=-1, keepdims=True)
    exponent = jnp.where(in_segment, jnp.exp(masked - highest), 0.0)
    row_total = jnp.sum(exponent, axis=-1, keepdims=True)
    probs_low = (exponent / row_total).astype(jnp.bfloat16)
    attended = jnp.einsum("hqk,khd->qhd", probs_low, value_rows, preferred_element_type=jnp.float32)
    return (attended, (highest + jnp.log(row_total))[..., 0])


def attend_back(packed):
    query_rows, key_rows, value_rows, segment, log_total, grad_mixed = packed
    scale = query_rows.shape[-1] ** (-0.5)
    raw_scores = jnp.einsum(
        "qhd,khd->hqk", query_rows, key_rows, preferred_element_type=jnp.float32
    )
    in_segment = segment_mask(segment)
    probs = jnp.where(in_segment, jnp.exp(raw_scores * scale - log_total[..., None]), 0.0)
    value_rows_gradient = jnp.einsum(
        "hqk,qhd->khd", probs.astype(jnp.bfloat16), grad_mixed, preferred_element_type=jnp.float32
    )
    grad_probs = jnp.einsum(
        "qhd,khd->hqk", grad_mixed, value_rows, preferred_element_type=jnp.float32
    )
    inner_sum = jnp.sum(probs * grad_probs, axis=-1, keepdims=True)
    grad_raw = (probs * (grad_probs - inner_sum) * scale).astype(jnp.bfloat16)
    query_rows_gradient = jnp.einsum(
        "hqk,khd->qhd", grad_raw, key_rows, preferred_element_type=jnp.float32
    )
    grad_keys = jnp.einsum("hqk,qhd->khd", grad_raw, query_rows, preferred_element_type=jnp.float32)
    return (
        query_rows_gradient.astype(jnp.bfloat16),
        grad_keys.astype(jnp.bfloat16),
        value_rows_gradient.astype(jnp.bfloat16),
    )


def local(
    inputs,
    segment_ids,
    cotangent,
    qkv_weight,
    out_weight,
    up_weight,
    down_weight,
    query_bias_vector,
    value_bias_vector,
    out_bias,
    gain_one,
    shift_one,
    up_bias,
    down_bias,
    gain_two,
    shift_two,
    query_down,
    query_up_weight,
    value_down,
    value_up_weight,
):
    dp, fsdp = lax.axis_size("dp"), lax.axis_size("fsdp")
    vector_shards = jnp.stack(
        [
            query_bias_vector,
            value_bias_vector,
            out_bias,
            gain_one,
            shift_one,
            down_bias,
            gain_two,
            shift_two,
        ],
        axis=1,
    )
    columns, wide = qkv_weight.shape[0], qkv_weight.shape[1]
    small = jnp.concatenate([vector_shards, up_bias.reshape(-1, columns).T], axis=1)
    small = jnp.pad(small, ((0, 0), (0, 128 - small.shape[1])))
    order = shard_order(dp, fsdp)
    first_full = assemble(order, *gather(jnp.concatenate([qkv_weight, small], axis=1), dp, fsdp))
    out_full = assemble(order, *gather(out_weight, dp, fsdp))
    up_full = assemble(order, *gather(up_weight, dp, fsdp))
    down_full = assemble(order, *gather(down_weight, dp, fsdp))
    qkv_full = first_full[:, :wide]
    vectors = first_full[:, wide : wide + 8].T.astype(jnp.float32)
    up_bias_full = first_full[:, wide + 8 : wide + 12].reshape(-1, columns, 4)
    up_bias_full = up_bias_full.transpose(0, 2, 1).reshape(-1)
    packs, seq_len, width = inputs.shape
    rows = packs * seq_len
    flat_in = inputs.reshape(rows, width)
    flat_float = flat_in.astype(jnp.float32)
    projected_rows = jnp.dot(flat_in, qkv_full, preferred_element_type=jnp.float32)
    query_rank_rows = jnp.dot(flat_in, query_down, preferred_element_type=jnp.float32)
    value_rank_rows = jnp.dot(flat_in, value_down, preferred_element_type=jnp.float32)
    query_up_weight_float = query_up_weight.astype(jnp.float32)
    value_up_weight_float = value_up_weight.astype(jnp.float32)
    query_rows = (
        projected_rows[:, :width]
        + vectors[0]
        + adapter_scale
        * jnp.dot(query_rank_rows, query_up_weight_float, precision=highest_precision_mode)
    ).astype(jnp.bfloat16)
    key_rows = projected_rows[:, width : 2 * width].astype(jnp.bfloat16)
    value_rows = (
        projected_rows[:, 2 * width :]
        + vectors[1]
        + adapter_scale
        * jnp.dot(value_rank_rows, value_up_weight_float, precision=highest_precision_mode)
    ).astype(jnp.bfloat16)
    head_shape = (packs, seq_len, HEADS, HEAD_DIM)
    queries_heads = query_rows.reshape(head_shape)
    keys_heads = key_rows.reshape(head_shape)
    values_heads = value_rows.reshape(head_shape)
    attended, log_total = lax.map(
        attend_pack, (queries_heads, keys_heads, values_heads, segment_ids)
    )
    attended_low = attended.reshape(rows, width).astype(jnp.bfloat16)
    hidden_one = (
        flat_float
        + jnp.dot(attended_low, out_full, preferred_element_type=jnp.float32)
        + vectors[2]
    )
    normed_one = layer_norm(hidden_one, vectors[3], vectors[4])
    upper = jnp.dot(
        normed_one.astype(jnp.bfloat16), up_full, preferred_element_type=jnp.float32
    ) + up_bias_full.astype(jnp.float32)
    activated, gelu_pull = jax.vjp(gelu_exact, upper)
    hidden_two = (
        normed_one
        + jnp.dot(activated.astype(jnp.bfloat16), down_full, preferred_element_type=jnp.float32)
        + vectors[5]
    )
    output = layer_norm(hidden_two, vectors[6], vectors[7]).astype(jnp.bfloat16)
    qkv_back, out_back, up_back, down_back = qkv_full, out_full, up_full, down_full
    gain_back_one, gain_back_two = vectors[3], vectors[6]
    grad_out = cotangent.reshape(rows, width).astype(jnp.float32)
    normed_again, pull_two = jax.vjp(partial(layer_norm, gain=gain_back_two, shift=0.0), hidden_two)
    (grad_two,) = pull_two(grad_out)
    grad_act = jnp.dot(
        grad_two.astype(jnp.bfloat16), down_back.T, preferred_element_type=jnp.float32
    )
    (grad_upper,) = gelu_pull(grad_act)
    grad_normed = grad_two + jnp.dot(
        grad_upper.astype(jnp.bfloat16), up_back.T, preferred_element_type=jnp.float32
    )
    first_again, pull_one = jax.vjp(partial(layer_norm, gain=gain_back_one, shift=0.0), hidden_one)
    (grad_one,) = pull_one(grad_normed)
    grad_mixed = jnp.dot(
        grad_one.astype(jnp.bfloat16), out_back.T, preferred_element_type=jnp.float32
    ).astype(jnp.bfloat16)
    query_rows_gradient, grad_keys, value_rows_gradient = lax.map(
        attend_back,
        (
            queries_heads,
            keys_heads,
            values_heads,
            segment_ids,
            log_total,
            grad_mixed.reshape(head_shape),
        ),
    )
    query_rows_gradient = query_rows_gradient.reshape(rows, width)
    value_rows_gradient = value_rows_gradient.reshape(rows, width)
    grad_project = jnp.concatenate(
        [query_rows_gradient, grad_keys.reshape(rows, width), value_rows_gradient], axis=1
    )
    query_rank_gradient = adapter_scale * jnp.dot(
        query_rows_gradient, query_up_weight.T, preferred_element_type=jnp.float32
    )
    value_rank_gradient = adapter_scale * jnp.dot(
        value_rows_gradient, value_up_weight.T, preferred_element_type=jnp.float32
    )
    grad_rows = grad_one + jnp.dot(grad_project, qkv_back.T, preferred_element_type=jnp.float32)
    grad_rows = grad_rows + jnp.dot(
        query_rank_gradient, query_down.astype(jnp.float32).T, precision=highest_precision_mode
    )
    grad_rows = grad_rows + jnp.dot(
        value_rank_gradient, value_down.astype(jnp.float32).T, precision=highest_precision_mode
    )
    term_query_up = jnp.dot(
        query_rank_rows.T,
        adapter_scale * query_rows_gradient.astype(jnp.float32),
        precision=highest_precision_mode,
    )
    term_value_up = jnp.dot(
        value_rank_rows.T,
        adapter_scale * value_rows_gradient.astype(jnp.float32),
        precision=highest_precision_mode,
    )
    term_query_down = jnp.dot(query_rank_gradient.T, flat_float, precision=highest_precision_mode)
    term_value_down = jnp.dot(value_rank_gradient.T, flat_float, precision=highest_precision_mode)
    terms = jnp.stack([term_query_down, term_query_up, term_value_down, term_value_up])
    terms = sum_everywhere(terms, dp, fsdp)
    sum_query_down, sum_query_up = terms[0].T, terms[1]
    sum_value_down, sum_value_up = terms[2].T, terms[3]
    return (
        output.reshape(packs, seq_len, width),
        grad_rows.reshape(packs, seq_len, width),
        sum_query_down,
        sum_query_up,
        sum_value_down,
        sum_value_up,
    )


def solution(mesh):
    in_specs = (
        P(("dp", "fsdp"), None, None),
        P(("dp", "fsdp"), None),
        P(("dp", "fsdp"), None, None),
        P(("dp", "fsdp"), None),
        P(("dp", "fsdp"), None),
        P(("dp", "fsdp"), None),
        P(("dp", "fsdp"), None),
        P(("dp", "fsdp")),
        P(("dp", "fsdp")),
        P(("dp", "fsdp")),
        P(("dp", "fsdp")),
        P(("dp", "fsdp")),
        P(("dp", "fsdp")),
        P(("dp", "fsdp")),
        P(("dp", "fsdp")),
        P(("dp", "fsdp")),
        P(),
        P(),
        P(),
        P(),
    )
    out_specs = (P(("dp", "fsdp"), None, None), P(("dp", "fsdp"), None, None), P(), P(), P(), P())
    return jax.shard_map(local, mesh=mesh, in_specs=in_specs, out_specs=out_specs, check_vma=False)
```

```python
import functools

import jax
import jax.numpy as jnp
from jax import lax
from jax.experimental import pallas as pl
from jax.experimental.pallas import tpu as pltpu
from jax.sharding import PartitionSpec as P

AXES = ("dp", "fsdp")
HEAD_DIM = 64
LANES = 128
LONG = 256
EPSILON = 1e-05
BF = jnp.bfloat16
F32 = jnp.float32
VMEM_LIMIT = 56 * 1024 * 1024
NT = (((1,), (1,)), ((), ()))
TN = (((0,), (0,)), ((), ()))


def log_two(number):
    return number.bit_length() - 1


def step_masks(dp, fsdp):
    z_count = dp // 2
    z_bits, f_bits = log_two(z_count), log_two(fsdp)
    x_bits = f_bits // 2
    z_zero = [1 << i for i in range(z_bits)]
    z_one = ([z_count - 1] + [1 << i for i in range(z_bits - 1)]) if z_bits else []
    x = [1 << i for i in range(x_bits)]
    y = [1 << i for i in range(x_bits, f_bits)]
    zero = [(m, 0) for m in z_zero] + [(0, m) for m in x + y]
    one = [(m, 0) for m in z_one] + [(0, m) for m in y + x]
    return list(zip(zero, one))


def step_pairs(dp, fsdp, steps):
    pairs = []
    for d in range(dp):
        mz, mf = steps[d % 2]
        for f in range(fsdp):
            target = ((((d // 2) ^ mz) * 2) + d % 2) * fsdp + (f ^ mf)
            pairs.append((d * fsdp + f, target))
    return pairs


def core_pairs(dp, fsdp):
    return [(d * fsdp + f, (d ^ 1) * fsdp + f) for d in range(dp) for f in range(fsdp)]


def shard_offsets(steps, core):
    masks = [(0, 0)]
    for step in steps:
        mz, mf = step[core]
        masks = masks + [(z ^ mz, f ^ mf) for z, f in masks]
    return masks


def shard_order(dp, fsdp):
    steps = step_masks(dp, fsdp)
    tables = [jnp.array(shard_offsets(steps, core), jnp.int32) for core in (0, 1)]
    d, f = lax.axis_index("dp"), lax.axis_index("fsdp")
    z, core = d // 2, d % 2
    mine = jnp.where(core == 0, tables[0], tables[1])
    other = jnp.where(core == 0, tables[1], tables[0])
    first = ((z ^ mine[:, 0]) * 2 + core) * fsdp + (f ^ mine[:, 1])
    second = ((z ^ other[:, 0]) * 2 + (1 - core)) * fsdp + (f ^ other[:, 1])
    return jnp.concatenate([first, second])


def gather(shard, dp, fsdp):
    buffer = shard[None]
    for steps in step_masks(dp, fsdp):
        got = lax.ppermute(buffer, AXES, step_pairs(dp, fsdp, steps))
        buffer = jnp.concatenate([buffer, got], axis=0)
    return buffer, lax.ppermute(buffer, AXES, core_pairs(dp, fsdp))


def sum_everywhere(value, dp, fsdp):
    value = value + lax.ppermute(value, AXES, core_pairs(dp, fsdp))
    for steps in step_masks(dp, fsdp):
        value = value + lax.ppermute(value, AXES, step_pairs(dp, fsdp, (steps[0], steps[0])))
    return value


def dot(left, right, dims=(((1,), (0,)), ((), ()))):
    return lax.dot_general(left, right, dims, preferred_element_type=F32)


def two_terms(value):
    high = value.astype(BF)
    return jnp.concatenate([high, (value - high.astype(F32)).astype(BF)], axis=1)


def fetch_start(order_ref, own, other, full, sems):
    half = own.shape[0]
    for place in range(2 * half):
        source = own.at[place] if place < half else other.at[place - half]
        pltpu.make_async_copy(source, full.at[order_ref[place]], sems.at[place]).start()


def fetch_wait(order_ref, own, other, full, sems):
    half = own.shape[0]
    for place in range(2 * half):
        source = own.at[place] if place < half else other.at[place - half]
        pltpu.make_async_copy(source, full.at[order_ref[place]], sems.at[place]).wait()


def matrix(full):
    places, rows, width = full.shape
    return full[...].reshape(places * rows, width)


def prepare_kernel(start_ref, x_ref, cot_ref, seg_ref, x_out, cot_out, bias_out):
    start = start_ref[pl.program_id(0)]
    rows = x_ref.shape[0]
    here = lax.broadcasted_iota(jnp.int32, (rows, rows), 0)
    there = lax.broadcasted_iota(jnp.int32, (rows, rows), 1)
    source = here + start
    source = jnp.where(source >= rows, source - rows, source)
    turn = jnp.where(there == source, 1.0, 0.0).astype(BF)
    x_out[...] = dot(turn, x_ref[...]).astype(BF)
    cot_out[...] = dot(turn, cot_ref[...]).astype(BF)
    segments = jnp.broadcast_to(seg_ref[0], (LANES, rows)).astype(BF)
    across = dot(segments, turn, NT)[:1, LONG:]
    down = dot(turn, segments, NT)[LONG:, :1]
    bias_out[0] = jnp.where(down == across, 0.0, -1e30)


def project_kernel(order_ref, x_ref, own, other, down_ref, up_ref, q_out, k_out, v_out, a_out, small_out, full, sems):
    @pl.when(pl.program_id(0) == 0)
    def _():
        fetch_start(order_ref, own, other, full, sems)
        fetch_wait(order_ref, own, other, full, sems)
        width = full.shape[2] - LANES
        eye = jnp.where(
            lax.broadcasted_iota(jnp.int32, (LANES, LANES), 0)
            == lax.broadcasted_iota(jnp.int32, (LANES, LANES), 1),
            1.0,
            0.0,
        ).astype(BF)
        small = full[:, :, width:].reshape(full.shape[0] * full.shape[1], LANES)
        small_out[...] = dot(eye, small, NT)[:16]

    x = x_ref[...]
    width = x.shape[1]
    weight = matrix(full)
    a = dot(x, down_ref[...])
    a_out[...] = a
    a_two = two_terms(a)
    q = dot(x, weight[:, :width]) + dot(a_two, up_ref[:, :width]) + small_out[0:1]
    q_out[...] = q.astype(BF)
    k_out[...] = dot(x, weight[:, width : 2 * width]).astype(BF)
    v = dot(x, weight[:, 2 * width : 3 * width]) + dot(a_two, up_ref[:, width:]) + small_out[1:2]
    v_out[...] = v.astype(BF)


def attend_kernel(q_ref, k_ref, v_ref, bias_ref, o_ref):
    lane = lax.broadcasted_iota(jnp.int32, (1, LANES), 1) < HEAD_DIM
    for block in (0, 1):
        rows = pl.ds(block * LONG, LONG)
        q, k, v = q_ref[rows, :], k_ref[rows, :], v_ref[rows, :]
        q = q * BF(HEAD_DIM**-0.5)
        zero = jnp.zeros_like(q)
        mixed = []
        for head in (0, 1):
            q_head = jnp.where(lane, q, zero) if head == 0 else jnp.where(lane, zero, q)
            scores = dot(q_head, k, NT)
            if block == 1:
                scores = scores + bias_ref[0]
            highest = jnp.max(scores, axis=1, keepdims=True)
            exponent = jnp.exp(scores - highest)
            total = jnp.sum(exponent, axis=1, keepdims=True)
            mixed.append(dot((exponent * (1.0 / total)).astype(BF), v))
        o_ref[rows, :] = jnp.where(lane, mixed[0], mixed[1]).astype(BF)


def attend_back_kernel(q_ref, k_ref, v_ref, g_ref, bias_ref, dq_ref, dk_ref, dv_ref):
    lane = lax.broadcasted_iota(jnp.int32, (1, LANES), 1) < HEAD_DIM
    scale = HEAD_DIM**-0.5
    for block in (0, 1):
        rows = pl.ds(block * LONG, LONG)
        q, k, v, g = q_ref[rows, :], k_ref[rows, :], v_ref[rows, :], g_ref[rows, :]
        zero = jnp.zeros_like(q)
        dq, dk, dv = [], [], []
        for head in (0, 1):
            pick = (lambda t: jnp.where(lane, t, zero)) if head == 0 else (lambda t: jnp.where(lane, zero, t))
            k_head = pick(k)
            scores = dot(k_head * BF(scale), q, NT)
            if block == 1:
                scores = scores + bias_ref[0]
            highest = jnp.max(scores, axis=0, keepdims=True)
            exponent = jnp.exp(scores - highest)
            total = jnp.sum(exponent, axis=0, keepdims=True)
            probs = exponent * (1.0 / total)
            dv.append(dot(probs.astype(BF), g))
            product = probs * dot(pick(v), g, NT)
            inner = jnp.sum(product, axis=0, keepdims=True)
            raw = ((product - probs * inner) * scale).astype(BF)
            dk.append(dot(raw, q))
            dq.append(dot(raw, k, TN))
        dq_ref[rows, :] = jnp.where(lane, dq[0], dq[1]).astype(BF)
        dk_ref[rows, :] = jnp.where(lane, dk[0], dk[1]).astype(BF)
        dv_ref[rows, :] = jnp.where(lane, dv[0], dv[1]).astype(BF)


TAIL_SHIFT = 0.28
TAIL = (
    0.11652168782509324,
    0.06749112571608445,
    0.2689240038768132,
    -0.2370103807862627,
    0.3898842701077009,
    -0.1058107160195692,
)


def gelu_and_slope(u):
    bell = jnp.exp(u * u * -0.5)
    t = 1.0 / (1.0 + TAIL_SHIFT * jnp.abs(u))
    series = jnp.full_like(u, TAIL[5])
    for coefficient in TAIL[4::-1]:
        series = series * t + coefficient
    tail = bell * (series * t)
    phi = jnp.where(u >= 0.0, 1.0 - tail, tail)
    return u * phi, phi + u * bell * 0.3989422804014327


def normalise(rows):
    centred = rows - jnp.mean(rows, axis=1, keepdims=True)
    variance = jnp.mean(centred * centred, axis=1, keepdims=True)
    inverse = lax.rsqrt(variance + EPSILON)
    return centred * inverse, inverse


def normalise_back(grad, y, inverse):
    mean = jnp.mean(grad, axis=1, keepdims=True)
    along = jnp.mean(grad * y, axis=1, keepdims=True)
    return inverse * (grad - mean - y * along)


CHUNK = 512


def upper_kernel(
    order_ref, o_ref, x_ref, small_ref, bias_ref, out_own, out_other, up_own, up_other,
    y_out, inverse_out, act_out, slope_out, out_full, up_full, out_sems, up_sems,
):
    first = pl.program_id(0) == 0

    @pl.when(first)
    def _():
        fetch_start(order_ref, out_own, out_other, out_full, out_sems)
        fetch_start(order_ref, up_own, up_other, up_full, up_sems)
        fetch_wait(order_ref, out_own, out_other, out_full, out_sems)

    hidden = x_ref[...].astype(F32) + dot(o_ref[...], matrix(out_full)) + small_ref[2:3]
    y, inverse = normalise(hidden)
    y_out[...] = y
    inverse_out[...] = jnp.broadcast_to(inverse, inverse_out.shape)
    normed = (y * small_ref[3:4] + small_ref[4:5]).astype(BF)

    @pl.when(first)
    def _():
        fetch_wait(order_ref, up_own, up_other, up_full, up_sems)

    for at in range(0, act_out.shape[1], CHUNK):
        columns = slice(at, at + CHUNK)
        weight = up_full[:, :, columns].reshape(-1, CHUNK)
        u = dot(normed, weight) + bias_ref[:, columns]
        act, slope = gelu_and_slope(u)
        act_out[:, columns] = act.astype(BF)
        slope_out[:, columns] = slope


def turn_back(scratch, out_ref, start, value):
    block = pl.program_id(1)
    scratch[pl.ds(pl.multiple_of(block * LONG, LONG), LONG), :] = value

    @pl.when(block == 1)
    def _():
        out_ref[0] = pltpu.roll(scratch[...], start, 0).astype(out_ref.dtype)


def lower_kernel(
    order_ref, start_ref, act_ref, slope_ref, y_ref, inverse_ref, cot_ref, small_ref,
    down_own, down_other, up_own, up_other, out_own, out_other,
    output_ref, dh_out, do_out,
    down_full, up_full, out_full, down_sems, up_sems, out_sems, scratch,
):
    first = (pl.program_id(0) == 0) & (pl.program_id(1) == 0)

    @pl.when(first)
    def _():
        fetch_start(order_ref, down_own, down_other, down_full, down_sems)
        fetch_start(order_ref, up_own, up_other, up_full, up_sems)
        fetch_start(order_ref, out_own, out_other, out_full, out_sems)
        fetch_wait(order_ref, down_own, down_other, down_full, down_sems)

    y_one = y_ref[...]
    normed = y_one * small_ref[3:4] + small_ref[4:5]
    hidden = normed + dot(act_ref[...], matrix(down_full)) + small_ref[5:6]
    y_two, inverse_two = normalise(hidden)
    turn_back(scratch, output_ref, start_ref[pl.program_id(0)], y_two * small_ref[6:7] + small_ref[7:8])
    grad_two = normalise_back(cot_ref[...].astype(F32) * small_ref[6:7], y_two, inverse_two)
    grad_low = grad_two.astype(BF)

    @pl.when(first)
    def _():
        fetch_wait(order_ref, up_own, up_other, up_full, up_sems)
        fetch_wait(order_ref, out_own, out_other, out_full, out_sems)

    grad_normed = grad_two
    per = down_full.shape[1]
    for at in range(0, act_ref.shape[1], CHUNK * 3 // 2):
        size = CHUNK * 3 // 2
        columns = slice(at, at + size)
        weight = down_full[at // per : (at + size) // per].reshape(size, -1)
        grad_upper = (dot(grad_low, weight, NT) * slope_ref[:, columns]).astype(BF)
        grad_normed = grad_normed + dot(grad_upper, up_full[:, :, columns].reshape(-1, size), NT)
    grad_one = normalise_back(grad_normed * small_ref[3:4], y_one, inverse_ref[:, :1])
    dh_out[...] = grad_one
    do_out[...] = dot(grad_one.astype(BF), matrix(out_full), NT).astype(BF)


def adapter_kernel(x_ref, a_ref, dq_ref, dv_ref, up_ref, e_out, terms_ref):
    width = x_ref.shape[1]
    dq, dv = dq_ref[...], dv_ref[...]
    e = dot(dq, up_ref[:LANES, :width], NT) + dot(dv, up_ref[:LANES, width:], NT)
    e_two = two_terms(e)
    e_out[...] = e_two
    a_two = two_terms(a_ref[...])
    down = dot(e_two, x_ref[...], TN)
    up_q, up_v = dot(a_two, dq, TN) * 2.0, dot(a_two, dv, TN) * 2.0
    down, up_q, up_v = (t[:LANES] + t[LANES:] for t in (down, up_q, up_v))
    terms_ref[0:8] = down[0:8]
    terms_ref[8:16] = up_q[0:8]
    terms_ref[16:24] = down[8:16]
    terms_ref[24:32] = up_v[8:16]


def input_kernel(
    order_ref, start_ref, dh_ref, dq_ref, dk_ref, dv_ref, e_ref, down_ref, own, other,
    grad_ref, full, sems, scratch,
):
    first = (pl.program_id(0) == 0) & (pl.program_id(1) == 0)

    @pl.when(first)
    def _():
        fetch_start(order_ref, own, other, full, sems)
        fetch_wait(order_ref, own, other, full, sems)

    weight = matrix(full)
    width = dh_ref.shape[1]
    grad = dh_ref[...] + dot(e_ref[...], down_ref[...], NT)
    grad = grad + dot(dq_ref[...], weight[:, :width], NT)
    grad = grad + dot(dk_ref[...], weight[:, width : 2 * width], NT)
    grad = grad + dot(dv_ref[...], weight[:, 2 * width : 3 * width], NT)
    turn_back(scratch, grad_ref, start_ref[pl.program_id(0)], grad)


def shape(dims, dtype):
    return jax.ShapeDtypeStruct(dims, dtype)


ANYWHERE = pl.BlockSpec(memory_space=pl.ANY)


def call(kernel, name, grid, prefetch, in_specs, out_specs, out_shape, scratch=()):
    return pl.pallas_call(
        kernel,
        out_shape=out_shape,
        grid_spec=pltpu.PrefetchScalarGridSpec(
            num_scalar_prefetch=prefetch,
            grid=grid,
            in_specs=in_specs,
            out_specs=out_specs,
            scratch_shapes=list(scratch),
        ),
        compiler_params=pltpu.CompilerParams(
            vmem_limit_bytes=VMEM_LIMIT, dimension_semantics=("arbitrary",) * len(grid)
        ),
        name=name,
    )


def full_scratch(buffers):
    places, rows, width = buffers[0].shape
    return pltpu.VMEM((2 * places, rows, width), BF), pltpu.SemaphoreType.DMA((2 * places,))


def whole(array):
    return pl.BlockSpec(array.shape, lambda *_: (0,) * array.ndim)


def prepare(start, inputs, cotangent, segment_ids):
    packs, seq, width = inputs.shape
    rows = packs * seq
    block = pl.BlockSpec((seq, width), lambda i, s: (i, 0))
    return call(
        prepare_kernel, "prepare", (packs,), 1,
        [block, block, pl.BlockSpec((1, 1, seq), lambda i, s: (i, 0, 0))],
        [block, block, pl.BlockSpec((1, LONG, LONG), lambda i, s: (i, 0, 0))],
        [shape((rows, width), BF), shape((rows, width), BF), shape((packs, LONG, LONG), F32)],
    )(start, inputs.reshape(rows, width), cotangent.reshape(rows, width), segment_ids.astype(F32)[:, None])


def project(order, x, buffers, adapter_down, adapter_up):
    rows, width = x.shape
    tile = pl.BlockSpec((LONG, width), lambda i, o: (i, 0))
    return call(
        project_kernel, "project", (rows // LONG,), 1,
        [tile, ANYWHERE, ANYWHERE, whole(adapter_down), whole(adapter_up)],
        [tile, tile, tile, pl.BlockSpec((LONG, LANES), lambda i, o: (i, 0)), pl.BlockSpec((16, width), lambda i, o: (0, 0))],
        [shape((rows, width), BF)] * 3 + [shape((rows, LANES), F32), shape((16, width), F32)],
        full_scratch(buffers),
    )(order, x, *buffers, adapter_down, adapter_up)


def attend(q, k, v, bias):
    rows, width = q.shape
    packs = bias.shape[0]
    block = pl.BlockSpec((rows // packs, LANES), lambda p, h: (p, h))
    return call(
        attend_kernel, "attend", (packs, width // LANES), 0,
        [block, block, block, pl.BlockSpec((1, LONG, LONG), lambda p, h: (p, 0, 0))],
        block, shape((rows, width), BF),
    )(q, k, v, bias)


def attend_back(q, k, v, g, bias):
    rows, width = q.shape
    packs = bias.shape[0]
    block = pl.BlockSpec((rows // packs, LANES), lambda p, h: (p, h))
    return call(
        attend_back_kernel, "attend_back", (packs, width // LANES), 0,
        [block] * 4 + [pl.BlockSpec((1, LONG, LONG), lambda p, h: (p, 0, 0))],
        [block] * 3, [shape((rows, width), BF)] * 3,
    )(q, k, v, g, bias)


def upper(order, mixed, x, small, up_bias, out_buffers, up_buffers):
    rows, width = x.shape
    hidden = up_bias.shape[1]
    tile = pl.BlockSpec((LONG, width), lambda i, o: (i, 0))
    wide = pl.BlockSpec((LONG, hidden), lambda i, o: (i, 0))
    (out_full, out_sems), (up_full, up_sems) = full_scratch(out_buffers), full_scratch(up_buffers)
    return call(
        upper_kernel, "upper", (rows // LONG,), 1,
        [tile, tile, whole(small), whole(up_bias)] + [ANYWHERE] * 4,
        [tile, pl.BlockSpec((LONG, LANES), lambda i, o: (i, 0)), wide, wide],
        [shape((rows, width), F32), shape((rows, LANES), F32), shape((rows, hidden), BF), shape((rows, hidden), F32)],
        [out_full, up_full, out_sems, up_sems],
    )(order, mixed, x, small, up_bias, *out_buffers, *up_buffers)


def lower(order, start, act, slope, y, inverse, cot, small, down_buffers, up_buffers, out_buffers):
    rows, width = y.shape
    packs, hidden = start.shape[0], act.shape[1]
    tile = pl.BlockSpec((LONG, width), lambda p, b, *_: (2 * p + b, 0))
    wide = pl.BlockSpec((LONG, hidden), lambda p, b, *_: (2 * p + b, 0))
    scratch = [full_scratch(b) for b in (down_buffers, up_buffers, out_buffers)]
    return call(
        lower_kernel, "lower", (packs, 2), 2,
        [wide, wide, tile, pl.BlockSpec((LONG, LANES), lambda p, b, *_: (2 * p + b, 0)), tile, whole(small)]
        + [ANYWHERE] * 6,
        [pl.BlockSpec((1, rows // packs, width), lambda p, b, *_: (p, 0, 0)), tile, tile],
        [shape((packs, rows // packs, width), BF), shape((rows, width), F32), shape((rows, width), BF)],
        [s[0] for s in scratch] + [s[1] for s in scratch] + [pltpu.VMEM((2 * LONG, width), F32)],
    )(order, start, act, slope, y, inverse, cot, small, *down_buffers, *up_buffers, *out_buffers)


def adapter_terms(x, a, dq, dv, adapter_up):
    rows, width = x.shape
    return call(
        adapter_kernel, "adapter", (1,), 0,
        [whole(t) for t in (x, a, dq, dv, adapter_up)],
        [pl.BlockSpec((rows, 2 * LANES), lambda i: (0, 0)), pl.BlockSpec((32, width), lambda i: (0, 0))],
        [shape((rows, 2 * LANES), BF), shape((32, width), F32)],
    )(x, a, dq, dv, adapter_up)


def input_gradient(order, start, dh, dq, dk, dv, e, adapter_down, buffers):
    rows, width = dh.shape
    packs = start.shape[0]
    tile = pl.BlockSpec((LONG, width), lambda p, b, *_: (2 * p + b, 0))
    return call(
        input_kernel, "input_gradient", (packs, 2), 2,
        [tile, tile, tile, tile, pl.BlockSpec((LONG, 2 * LANES), lambda p, b, *_: (2 * p + b, 0)), whole(adapter_down)]
        + [ANYWHERE] * 2,
        pl.BlockSpec((1, rows // packs, width), lambda p, b, *_: (p, 0, 0)),
        shape((packs, rows // packs, width), F32),
        list(full_scratch(buffers)) + [pltpu.VMEM((2 * LONG, width), F32)],
    )(order, start, dh, dq, dk, dv, e, adapter_down, *buffers)


def pack_adapters(query_down, query_up, value_down, value_up):
    width, rank = query_down.shape
    down = jnp.concatenate([query_down, value_down], axis=1)
    down = jnp.pad(down, ((0, 0), (0, LANES - 2 * rank)))
    zeros = jnp.zeros_like(query_up)
    up = jnp.concatenate([
        jnp.concatenate([query_up, zeros], axis=1), jnp.concatenate([zeros, value_up], axis=1)
    ]) * BF(2.0)
    up = jnp.pad(up, ((0, LANES - 2 * rank), (0, 0)))
    return down, jnp.concatenate([down, down], axis=1), jnp.concatenate([up, up])


def document_start(segment_ids):
    ids = jnp.arange(4, dtype=jnp.int32)
    counts = jnp.sum((segment_ids[:, :, None] == ids).astype(jnp.int32), axis=1)
    before = jnp.cumsum(counts, axis=1) - counts
    return jnp.clip(jnp.sum(jnp.where(counts == LONG, before, 0), axis=1), 0, LONG)


def compute(order, inputs, segment_ids, cotangent, first, out, up, down, adapters):
    packs, seq, width = inputs.shape
    adapter_down, adapter_down_two, adapter_up = pack_adapters(*adapters)
    start = document_start(segment_ids)
    x, cot, bias = prepare(start, inputs, cotangent, segment_ids)
    q, k, v, a, small = project(order, x, first, adapter_down, adapter_up)
    per = first[0].shape[1]
    up_bias = small[8:12].reshape(4, -1, per).transpose(1, 0, 2).reshape(1, -1)
    mixed = attend(q, k, v, bias)
    y, inverse, act, slope = upper(order, mixed, x, small, up_bias, out, up)
    output, dh, do = lower(order, start, act, slope, y, inverse, cot, small, down, up, out)
    dq, dk, dv = attend_back(q, k, v, do, bias)
    e, terms = adapter_terms(x, a, dq, dv, adapter_up)
    grad = input_gradient(order, start, dh, dq, dk, dv, e, adapter_down_two, first)
    return output, grad, terms


def first_shard(qkv_weight, vectors, up_bias):
    rows = qkv_weight.shape[0]
    small = jnp.concatenate([jnp.stack(vectors, axis=1), up_bias.reshape(-1, rows).T], axis=1)
    small = jnp.pad(small, ((0, 0), (0, LANES - small.shape[1])))
    return jnp.concatenate([qkv_weight, small], axis=1)


def local(
    inputs, segment_ids, cotangent, qkv_weight, out_weight, up_weight, down_weight,
    query_bias_vector, value_bias_vector, out_bias, gain_one, shift_one, up_bias, down_bias, gain_two, shift_two,
    query_down, query_up_weight, value_down, value_up_weight,
):
    dp, fsdp = lax.axis_size("dp"), lax.axis_size("fsdp")
    vectors = [
        query_bias_vector, value_bias_vector, out_bias, gain_one, shift_one, down_bias, gain_two, shift_two
    ]
    order = shard_order(dp, fsdp)
    first = gather(first_shard(qkv_weight, vectors, up_bias), dp, fsdp)
    out = gather(out_weight, dp, fsdp)
    up = gather(up_weight, dp, fsdp)
    down = gather(down_weight, dp, fsdp)
    output, grad, terms = compute(
        order, inputs, segment_ids, cotangent, first, out, up, down,
        (query_down, query_up_weight, value_down, value_up_weight),
    )
    terms = sum_everywhere(terms, dp, fsdp)
    rank = query_down.shape[1]
    return (
        output, grad,
        terms[:rank].T, terms[rank : 2 * rank], terms[2 * rank : 3 * rank].T, terms[3 * rank :],
    )


def solution(mesh):
    split = AXES
    in_specs = (
        (P(split, None, None), P(split, None), P(split, None, None))
        + (P(split, None),) * 4
        + (P(split),) * 9
        + (P(),) * 4
    )
    out_specs = (P(split, None, None), P(split, None, None), P(), P(), P(), P())
    return jax.shard_map(local, mesh=mesh, in_specs=in_specs, out_specs=out_specs, check_vma=False)
```

```python
import functools

import jax
import jax.numpy as jnp
from jax import lax
from jax.experimental import pallas as pl
from jax.experimental.pallas import tpu as pltpu
from jax.sharding import PartitionSpec as P

AXES = ("dp", "fsdp")
HEAD_DIM = 64
LANES = 128
LONG = 256
EPSILON = 1e-05
BF = jnp.bfloat16
F32 = jnp.float32
VMEM_LIMIT = 56 * 1024 * 1024
NT = (((1,), (1,)), ((), ()))
TN = (((0,), (0,)), ((), ()))


def log_two(number):
    return number.bit_length() - 1


def fsdp_masks(fsdp):
    bits = log_two(fsdp)
    x, y = [1 << i for i in range(bits // 2)], [1 << i for i in range(bits // 2, bits)]
    return list(zip(x + y, y + x)) if len(x) == len(y) else [(m, m) for m in x + y]


def pairs_of(dp, fsdp, z_masks, f_masks):
    pairs = []
    for d in range(dp):
        for f in range(fsdp):
            target = ((((d // 2) ^ z_masks[d % 2]) * 2) + d % 2) * fsdp + (f ^ f_masks[d % 2])
            pairs.append((d * fsdp + f, target))
    return pairs


def core_pairs(dp, fsdp):
    return [(d * fsdp + f, (d ^ 1) * fsdp + f) for d in range(dp) for f in range(fsdp)]


def shard_order(dp, fsdp):
    masks = [(0, 0)]
    for pair in fsdp_masks(fsdp):
        masks = masks + [(m[0] ^ pair[0], m[1] ^ pair[1]) for m in masks]
    d, f = lax.axis_index("dp"), lax.axis_index("fsdp")
    z, core = d // 2, d % 2
    places = []
    for owner in (core, 1 - core):
        f_mask = jnp.where(owner == 0, jnp.array([m[0] for m in masks]), jnp.array([m[1] for m in masks]))
        shard = ((z ^ jnp.arange(dp // 2)[None, :]) * 2 + owner) * fsdp + (f ^ f_mask[:, None])
        places.append(shard.reshape(-1))
    return jnp.concatenate(places).astype(jnp.int32)


def along_z(shard, dp, fsdp):
    got = [shard[None]]
    for mask in range(1, dp // 2):
        got.append(lax.ppermute(shard[None], AXES, pairs_of(dp, fsdp, (mask, mask), (0, 0))))
    return jnp.concatenate(got, axis=0)


def spread(column, dp, fsdp):
    pieces = [column]
    for masks in fsdp_masks(fsdp):
        pieces = pieces + [lax.ppermute(p, AXES, pairs_of(dp, fsdp, (0, 0), masks)) for p in pieces]
    return pieces + [lax.ppermute(p, AXES, core_pairs(dp, fsdp)) for p in pieces]


def sum_everywhere(value, dp, fsdp):
    z_count = dp // 2
    zero = [1 << i for i in range(log_two(z_count))]
    one = ([z_count - 1] + zero[:-1]) if zero else []
    for masks in zip(zero, one):
        value = value + lax.ppermute(value, AXES, pairs_of(dp, fsdp, masks, (0, 0)))
    for masks in fsdp_masks(fsdp):
        value = value + lax.ppermute(value, AXES, pairs_of(dp, fsdp, (0, 0), masks))
    return value + lax.ppermute(value, AXES, core_pairs(dp, fsdp))


def after(value, *others):
    return lax.optimization_barrier((value,) + others)[0]


def dot(left, right, dims=(((1,), (0,)), ((), ()))):
    return lax.dot_general(left, right, dims, preferred_element_type=F32)


def two_terms(value):
    high = value.astype(BF)
    return jnp.concatenate([high, (value - high.astype(F32)).astype(BF)], axis=1)


def fetches(order_ref, pieces, at, full, sems):
    place = 0
    for piece in pieces:
        for row in range(piece.shape[0]):
            source = piece.at[row, :, pl.ds(at, full.shape[2])]
            yield pltpu.make_async_copy(source, full.at[order_ref[place]], sems.at[place])
            place += 1


def fetch_start(*args):
    for copy in fetches(*args):
        copy.start()


def fetch_wait(*args):
    for copy in fetches(*args):
        copy.wait()


def matrix(full):
    places, rows, width = full.shape
    return full[...].reshape(places * rows, width)


def identity(size):
    here = lax.broadcasted_iota(jnp.int32, (size, size), 0)
    return jnp.where(here == lax.broadcasted_iota(jnp.int32, (size, size), 1), 1.0, 0.0).astype(BF)


def pack_kernel(weight_ref, *refs):
    vectors, bias_ref, out_ref = refs[:-2], refs[-2], refs[-1]
    rows, width = weight_ref.shape
    out_ref[:, :width] = weight_ref[...]
    lines = [v[...].reshape(1, rows) for v in vectors]
    lines = lines + [bias_ref[:, at : at + rows] for at in range(0, bias_ref.shape[1], rows)]
    lines = jnp.concatenate(lines + [jnp.zeros_like(lines[0])] * (-len(lines) % 16), axis=0)
    eye = identity(LANES)[: lines.shape[0]]
    out_ref[:, width:] = dot(lines, eye, TN).astype(BF)


def prepare_kernel(start_ref, x_ref, cot_ref, seg_ref, x_out, cot_out, bias_out):
    start = start_ref[pl.program_id(0)]
    rows = x_ref.shape[0]
    here = lax.broadcasted_iota(jnp.int32, (rows, rows), 0)
    there = lax.broadcasted_iota(jnp.int32, (rows, rows), 1)
    source = here + start
    source = jnp.where(source >= rows, source - rows, source)
    turn = jnp.where(there == source, 1.0, 0.0).astype(BF)
    x_out[...] = dot(turn, x_ref[...]).astype(BF)
    cot_out[...] = dot(turn, cot_ref[...]).astype(BF)
    segments = jnp.broadcast_to(seg_ref[0], (LANES, rows)).astype(BF)
    across = dot(segments, turn, NT)[:1, LONG:]
    down = dot(turn, segments, NT)[LONG:, :1]
    bias_out[0] = jnp.where(down == across, 0.0, -1e30)


def project_kernel(count, order_ref, x_ref, down_ref, up_ref, *refs):
    pieces, (q_out, k_out, v_out, a_out, small_out, full, sems) = refs[:count], refs[count:]

    @pl.when(pl.program_id(0) == 0)
    def _():
        fetch_start(order_ref, pieces, 0, full, sems)
        fetch_wait(order_ref, pieces, 0, full, sems)
        width = full.shape[2] - LANES
        small = full[:, :, width:].reshape(full.shape[0] * full.shape[1], LANES)
        small_out[...] = dot(identity(LANES), small, NT)[:16]

    x = x_ref[...]
    width = x.shape[1]
    weight = matrix(full)
    a = dot(x, down_ref[...])
    a_out[...] = a
    a_two = two_terms(a)
    q = dot(x, weight[:, :width]) + dot(a_two, up_ref[:, :width]) + small_out[0:1]
    q_out[...] = q.astype(BF)
    k_out[...] = dot(x, weight[:, width : 2 * width]).astype(BF)
    v = dot(x, weight[:, 2 * width : 3 * width]) + dot(a_two, up_ref[:, width:]) + small_out[1:2]
    v_out[...] = v.astype(BF)


def heads_apart(pair, lane):
    zero = jnp.zeros_like(pair)
    return jnp.concatenate([jnp.where(lane, pair, zero), jnp.where(lane, zero, pair)], axis=0)


def softmax_down(scores, bias):
    if bias is not None:
        scores = scores + bias
    exponent = jnp.exp(scores - jnp.max(scores, axis=0, keepdims=True))
    return exponent * (1.0 / jnp.sum(exponent, axis=0, keepdims=True))


def attend_kernel(q_ref, k_ref, v_ref, bias_ref, o_ref):
    lane = lax.broadcasted_iota(jnp.int32, (1, LANES), 1) < HEAD_DIM
    for at in range(0, q_ref.shape[1], LANES):
        for block in (0, 1):
            here = (pl.ds(block * LONG, LONG), pl.ds(at, LANES))
            bias = bias_ref[0] if block == 1 else None
            scores = dot(heads_apart(k_ref[here], lane) * BF(HEAD_DIM**-0.5), q_ref[here], NT)
            probs = [softmax_down(scores[h : h + LONG], bias).astype(BF) for h in (0, LONG)]
            mixed = dot(jnp.concatenate(probs, axis=0), heads_apart(v_ref[here], lane), TN)
            o_ref[here] = mixed.astype(BF)


def attend_back_kernel(q_ref, k_ref, v_ref, g_ref, bias_ref, dq_ref, dk_ref, dv_ref):
    lane = lax.broadcasted_iota(jnp.int32, (1, LANES), 1) < HEAD_DIM
    scale = BF(HEAD_DIM**-0.5)
    for at in range(0, q_ref.shape[1], LANES):
        for block in (0, 1):
            here = (pl.ds(block * LONG, LONG), pl.ds(at, LANES))
            bias = bias_ref[0] if block == 1 else None
            q, g = q_ref[here], g_ref[here]
            k_apart = heads_apart(k_ref[here], lane)
            scores = dot(k_apart * scale, q, NT)
            grad_probs = dot(heads_apart(v_ref[here], lane) * scale, g, NT)
            low, raw = [], []
            for h in (0, LONG):
                probs = softmax_down(scores[h : h + LONG], bias)
                low.append(probs.astype(BF))
                product = probs * grad_probs[h : h + LONG]
                inner = jnp.sum(product, axis=0, keepdims=True)
                raw.append((product - probs * inner).astype(BF))
            dv_ref[here] = dot(jnp.concatenate(low, axis=1), heads_apart(g, lane)).astype(BF)
            dk_ref[here] = dot(jnp.concatenate(raw, axis=1), heads_apart(q, lane)).astype(BF)
            dq_ref[here] = dot(jnp.concatenate(raw, axis=0), k_apart, TN).astype(BF)


TAIL_SHIFT = 0.28
TAIL = (
    0.11652168782509324,
    0.06749112571608445,
    0.2689240038768132,
    -0.2370103807862627,
    0.3898842701077009,
    -0.1058107160195692,
)


def gelu_and_slope(u):
    bell = jnp.exp(u * u * -0.5)
    t = 1.0 / (1.0 + TAIL_SHIFT * jnp.abs(u))
    series = jnp.full_like(u, TAIL[5])
    for coefficient in TAIL[4::-1]:
        series = series * t + coefficient
    tail = bell * (series * t)
    phi = jnp.where(u >= 0.0, 1.0 - tail, tail)
    return u * phi, phi + u * bell * 0.3989422804014327


def normalise(rows):
    centred = rows - jnp.mean(rows, axis=1, keepdims=True)
    variance = jnp.mean(centred * centred, axis=1, keepdims=True)
    inverse = lax.rsqrt(variance + EPSILON)
    return centred * inverse, inverse


def normalise_back(grad, y, inverse):
    mean = jnp.mean(grad, axis=1, keepdims=True)
    along = jnp.mean(grad * y, axis=1, keepdims=True)
    return inverse * (grad - mean - y * along)


CHUNK = 512


def upper_kernel(count, order_ref, o_ref, x_ref, small_ref, bias_ref, *refs):
    pieces, (y_out, inverse_out, act_out, slope_out, out_full, up_full, out_sems, up_sems) = refs[:count], refs[count:]
    first = pl.program_id(0) == 0
    split = out_full.shape[2]

    @pl.when(first)
    def _():
        fetch_start(order_ref, pieces, 0, out_full, out_sems)
        fetch_start(order_ref, pieces, split, up_full, up_sems)
        fetch_wait(order_ref, pieces, 0, out_full, out_sems)

    hidden = x_ref[...].astype(F32) + dot(o_ref[...], matrix(out_full)) + small_ref[2:3]
    y, inverse = normalise(hidden)
    y_out[...] = y
    inverse_out[...] = jnp.broadcast_to(inverse, inverse_out.shape)
    normed = (y * small_ref[3:4] + small_ref[4:5]).astype(BF)

    @pl.when(first)
    def _():
        fetch_wait(order_ref, pieces, split, up_full, up_sems)

    for at in range(0, act_out.shape[1], CHUNK):
        columns = slice(at, at + CHUNK)
        weight = up_full[:, :, columns].reshape(-1, CHUNK)
        u = dot(normed, weight) + bias_ref[:, columns]
        act, slope = gelu_and_slope(u)
        act_out[:, columns] = act.astype(BF)
        slope_out[:, columns] = slope


def turn_back(scratch, out_ref, start, value):
    block = pl.program_id(1)
    scratch[pl.ds(pl.multiple_of(block * LONG, LONG), LONG), :] = value

    @pl.when(block == 1)
    def _():
        out_ref[0] = pltpu.roll(scratch[...], start, 0).astype(out_ref.dtype)


def lower_kernel(
    count, order_ref, start_ref, act_ref, slope_ref, y_ref, inverse_ref, cot_ref, small_ref, *refs
):
    pieces, more = refs[:count], refs[count : 2 * count]
    output_ref, dh_out, do_out, down_full, up_full, out_full, down_sems, up_sems, out_sems, scratch = refs[2 * count :]
    first = (pl.program_id(0) == 0) & (pl.program_id(1) == 0)
    split = out_full.shape[2]

    @pl.when(first)
    def _():
        fetch_start(order_ref, pieces, 0, down_full, down_sems)
        fetch_start(order_ref, more, split, up_full, up_sems)
        fetch_start(order_ref, more, 0, out_full, out_sems)
        fetch_wait(order_ref, pieces, 0, down_full, down_sems)

    y_one = y_ref[...]
    normed = y_one * small_ref[3:4] + small_ref[4:5]
    hidden = normed + dot(act_ref[...], matrix(down_full)) + small_ref[5:6]
    y_two, inverse_two = normalise(hidden)
    turn_back(scratch, output_ref, start_ref[pl.program_id(0)], y_two * small_ref[6:7] + small_ref[7:8])
    grad_two = normalise_back(cot_ref[...].astype(F32) * small_ref[6:7], y_two, inverse_two)
    grad_low = grad_two.astype(BF)

    @pl.when(first)
    def _():
        fetch_wait(order_ref, more, split, up_full, up_sems)
        fetch_wait(order_ref, more, 0, out_full, out_sems)

    grad_normed = grad_two
    per = down_full.shape[1]
    for at in range(0, act_ref.shape[1], CHUNK * 3 // 2):
        size = CHUNK * 3 // 2
        columns = slice(at, at + size)
        weight = down_full[at // per : (at + size) // per].reshape(size, -1)
        grad_upper = (dot(grad_low, weight, NT) * slope_ref[:, columns]).astype(BF)
        grad_normed = grad_normed + dot(grad_upper, up_full[:, :, columns].reshape(-1, size), NT)
    grad_one = normalise_back(grad_normed * small_ref[3:4], y_one, inverse_ref[:, :1])
    dh_out[...] = grad_one
    do_out[...] = dot(grad_one.astype(BF), matrix(out_full), NT).astype(BF)


def adapter_kernel(x_ref, a_ref, dq_ref, dv_ref, up_ref, e_out, terms_ref):
    width = x_ref.shape[1]
    dq, dv = dq_ref[...], dv_ref[...]
    e = dot(dq, up_ref[:LANES, :width], NT) + dot(dv, up_ref[:LANES, width:], NT)
    e_two = two_terms(e)
    e_out[...] = e_two
    a_two = two_terms(a_ref[...])
    down = dot(e_two, x_ref[...], TN)
    up_q, up_v = dot(a_two, dq, TN) * 2.0, dot(a_two, dv, TN) * 2.0
    down, up_q, up_v = (t[:LANES] + t[LANES:] for t in (down, up_q, up_v))
    terms_ref[0:8] = down[0:8]
    terms_ref[8:16] = up_q[0:8]
    terms_ref[16:24] = down[8:16]
    terms_ref[24:32] = up_v[8:16]


def input_kernel(count, order_ref, start_ref, dh_ref, dq_ref, dk_ref, dv_ref, e_ref, down_ref, *refs):
    pieces, (grad_ref, full, sems, scratch) = refs[:count], refs[count:]
    first = (pl.program_id(0) == 0) & (pl.program_id(1) == 0)

    @pl.when(first)
    def _():
        fetch_start(order_ref, pieces, 0, full, sems)
        fetch_wait(order_ref, pieces, 0, full, sems)

    weight = matrix(full)
    width = dh_ref.shape[1]
    grad = dh_ref[...] + dot(e_ref[...], down_ref[...], NT)
    grad = grad + dot(dq_ref[...], weight[:, :width], NT)
    grad = grad + dot(dk_ref[...], weight[:, width : 2 * width], NT)
    grad = grad + dot(dv_ref[...], weight[:, 2 * width : 3 * width], NT)
    turn_back(scratch, grad_ref, start_ref[pl.program_id(0)], grad)


def shape(dims, dtype):
    return jax.ShapeDtypeStruct(dims, dtype)


ANYWHERE = pl.BlockSpec(memory_space=pl.ANY)


def call(kernel, name, grid, prefetch, in_specs, out_specs, out_shape, scratch=(), flops=0, moved=0):
    return pl.pallas_call(
        kernel,
        out_shape=out_shape,
        grid_spec=pltpu.PrefetchScalarGridSpec(
            num_scalar_prefetch=prefetch,
            grid=grid,
            in_specs=in_specs,
            out_specs=out_specs,
            scratch_shapes=list(scratch),
        ),
        compiler_params=pltpu.CompilerParams(
            vmem_limit_bytes=VMEM_LIMIT, dimension_semantics=("arbitrary",) * len(grid)
        ),
        cost_estimate=pl.CostEstimate(flops=flops, transcendentals=0, bytes_accessed=moved),
        name=name,
    )


def full_scratch(pieces, width):
    places = sum(p.shape[0] for p in pieces)
    return pltpu.VMEM((places, pieces[0].shape[1], width), BF), pltpu.SemaphoreType.DMA((places,))


def whole(array):
    return pl.BlockSpec(array.shape, lambda *_: (0,) * array.ndim)


def pack(weight, vectors, bias):
    rows, width = weight.shape
    operands = (weight, *[v.reshape(1, rows) for v in vectors], bias.reshape(1, -1))
    return call(
        pack_kernel, "pack", (1,), 0, [whole(t) for t in operands],
        pl.BlockSpec((rows, width + LANES), lambda i: (0, 0)), shape((rows, width + LANES), BF),
    )(*operands)


def prepare(start, inputs, cotangent, segment_ids):
    packs, seq, width = inputs.shape
    rows = packs * seq
    block = pl.BlockSpec((seq, width), lambda i, s: (i, 0))
    return call(
        prepare_kernel, "prepare", (packs,), 1,
        [block, block, pl.BlockSpec((1, 1, seq), lambda i, s: (i, 0, 0))],
        [block, block, pl.BlockSpec((1, LONG, LONG), lambda i, s: (i, 0, 0))],
        [shape((rows, width), BF), shape((rows, width), BF), shape((packs, LONG, LONG), F32)],
        flops=4 * rows * seq * width, moved=8 * rows * width,
    )(start, inputs.reshape(rows, width), cotangent.reshape(rows, width), segment_ids.astype(F32)[:, None])


def project(order, x, pieces, adapter_down, adapter_up):
    rows, width = x.shape
    tile = pl.BlockSpec((LONG, width), lambda i, o: (i, 0))
    return call(
        functools.partial(project_kernel, len(pieces)), "project", (rows // LONG,), 1,
        [tile, whole(adapter_down), whole(adapter_up)] + [ANYWHERE] * len(pieces),
        [tile, tile, tile, pl.BlockSpec((LONG, LANES), lambda i, o: (i, 0)), pl.BlockSpec((16, width), lambda i, o: (0, 0))],
        [shape((rows, width), BF)] * 3 + [shape((rows, LANES), F32), shape((16, width), F32)],
        full_scratch(pieces, pieces[0].shape[2]),
        flops=6 * rows * width * width, moved=8 * rows * width + 6 * width * width,
    )(order, x, adapter_down, adapter_up, *pieces)


def attend(q, k, v, bias):
    rows, width = q.shape
    packs = bias.shape[0]
    block = pl.BlockSpec((rows // packs, width), lambda p: (p, 0))
    return call(
        attend_kernel, "attend", (packs,), 0,
        [block, block, block, pl.BlockSpec((1, LONG, LONG), lambda p: (p, 0, 0))],
        block, shape((rows, width), BF),
        flops=16 * rows * width * LONG, moved=8 * rows * width,
    )(q, k, v, bias)


def attend_back(q, k, v, g, bias):
    rows, width = q.shape
    packs = bias.shape[0]
    block = pl.BlockSpec((rows // packs, width // 2), lambda p, h: (p, h))
    return call(
        attend_back_kernel, "attend_back", (packs, 2), 0,
        [block] * 4 + [pl.BlockSpec((1, LONG, LONG), lambda p, h: (p, 0, 0))],
        [block] * 3, [shape((rows, width), BF)] * 3,
        flops=40 * rows * width * LONG, moved=14 * rows * width,
    )(q, k, v, g, bias)


def upper(order, mixed, x, small, up_bias, pieces):
    rows, width = x.shape
    hidden = up_bias.shape[1]
    tile = pl.BlockSpec((LONG, width), lambda i, o: (i, 0))
    wide = pl.BlockSpec((LONG, hidden), lambda i, o: (i, 0))
    (out_full, out_sems), (up_full, up_sems) = full_scratch(pieces, width), full_scratch(pieces, hidden)
    return call(
        functools.partial(upper_kernel, len(pieces)), "upper", (rows // LONG,), 1,
        [tile, tile, whole(small), whole(up_bias)] + [ANYWHERE] * len(pieces),
        [tile, pl.BlockSpec((LONG, LANES), lambda i, o: (i, 0)), wide, wide],
        [shape((rows, width), F32), shape((rows, LANES), F32), shape((rows, hidden), BF), shape((rows, hidden), F32)],
        [out_full, up_full, out_sems, up_sems],
        flops=4 * rows * width * (width + 2 * hidden), moved=6 * rows * hidden,
    )(order, mixed, x, small, up_bias, *pieces)


def lower(order, start, act, slope, y, inverse, cot, small, pieces, more):
    rows, width = y.shape
    packs, hidden = start.shape[0], act.shape[1]
    tile = pl.BlockSpec((LONG, width), lambda p, b, *_: (2 * p + b, 0))
    wide = pl.BlockSpec((LONG, hidden), lambda p, b, *_: (2 * p + b, 0))
    scratch = [full_scratch(pieces, width), full_scratch(more, hidden), full_scratch(more, width)]
    return call(
        functools.partial(lower_kernel, len(pieces)), "lower", (packs, 2), 2,
        [wide, wide, tile, pl.BlockSpec((LONG, LANES), lambda p, b, *_: (2 * p + b, 0)), tile, whole(small)]
        + [ANYWHERE] * (2 * len(pieces)),
        [pl.BlockSpec((1, rows // packs, width), lambda p, b, *_: (p, 0, 0)), tile, tile],
        [shape((packs, rows // packs, width), BF), shape((rows, width), F32), shape((rows, width), BF)],
        [s[0] for s in scratch] + [s[1] for s in scratch] + [pltpu.VMEM((2 * LONG, width), F32)],
        flops=8 * rows * width * hidden, moved=6 * rows * hidden + 8 * rows * width,
    )(order, start, act, slope, y, inverse, cot, small, *pieces, *more)


def adapter_terms(x, a, dq, dv, adapter_up):
    rows, width = x.shape
    return call(
        adapter_kernel, "adapter", (1,), 0,
        [whole(t) for t in (x, a, dq, dv, adapter_up)],
        [pl.BlockSpec((rows, 2 * LANES), lambda i: (0, 0)), pl.BlockSpec((32, width), lambda i: (0, 0))],
        [shape((rows, 2 * LANES), BF), shape((32, width), F32)],
        flops=2048 * rows * width, moved=6 * rows * width,
    )(x, a, dq, dv, adapter_up)


def input_gradient(order, start, dh, dq, dk, dv, e, adapter_down, pieces):
    rows, width = dh.shape
    packs = start.shape[0]
    tile = pl.BlockSpec((LONG, width), lambda p, b, *_: (2 * p + b, 0))
    return call(
        functools.partial(input_kernel, len(pieces)), "input_gradient", (packs, 2), 2,
        [tile, tile, tile, tile, pl.BlockSpec((LONG, 2 * LANES), lambda p, b, *_: (2 * p + b, 0)), whole(adapter_down)]
        + [ANYWHERE] * len(pieces),
        pl.BlockSpec((1, rows // packs, width), lambda p, b, *_: (p, 0, 0)),
        shape((packs, rows // packs, width), F32),
        list(full_scratch(pieces, pieces[0].shape[2])) + [pltpu.VMEM((2 * LONG, width), F32)],
        flops=6 * rows * width * width, moved=14 * rows * width,
    )(order, start, dh, dq, dk, dv, e, adapter_down, *pieces)


def pack_adapters(query_down, query_up, value_down, value_up):
    width, rank = query_down.shape
    down = jnp.concatenate([query_down, value_down], axis=1)
    down = jnp.pad(down, ((0, 0), (0, LANES - 2 * rank)))
    zeros = jnp.zeros_like(query_up)
    up = jnp.concatenate([
        jnp.concatenate([query_up, zeros], axis=1), jnp.concatenate([zeros, value_up], axis=1)
    ]) * BF(2.0)
    up = jnp.pad(up, ((0, LANES - 2 * rank), (0, 0)))
    return down, jnp.concatenate([down, down], axis=1), jnp.concatenate([up, up])


def document_start(segment_ids):
    ids = jnp.arange(4, dtype=jnp.int32)
    counts = jnp.sum((segment_ids[:, :, None] == ids).astype(jnp.int32), axis=1)
    before = jnp.cumsum(counts, axis=1) - counts
    return jnp.clip(jnp.sum(jnp.where(counts == LONG, before, 0), axis=1), 0, LONG)


def compute(order, inputs, segment_ids, cotangent, first, second, third, adapters):
    adapter_down, adapter_down_two, adapter_up = pack_adapters(*adapters)
    start = document_start(segment_ids)
    x, cot, bias = prepare(start, inputs, cotangent, segment_ids)
    q, k, v, a, small = project(order, x, first, adapter_down, adapter_up)
    per = first[0].shape[1]
    up_bias = small[8:12].reshape(4, -1, per).transpose(1, 0, 2).reshape(1, -1)
    mixed = attend(q, k, v, bias)
    y, inverse, act, slope = upper(order, mixed, x, small, up_bias, second)
    output, dh, do = lower(order, start, act, slope, y, inverse, cot, small, third, second)
    dq, dk, dv = attend_back(q, k, v, do, bias)
    e, terms = adapter_terms(x, a, dq, dv, adapter_up)
    return output, terms, lambda: input_gradient(order, start, dh, dq, dk, dv, e, adapter_down_two, first)


def local(
    inputs, segment_ids, cotangent, qkv_weight, out_weight, up_weight, down_weight,
    query_bias_vector, value_bias_vector, out_bias, gain_one, shift_one, up_bias, down_bias, gain_two, shift_two,
    query_down, query_up_weight, value_down, value_up_weight,
):
    dp, fsdp = lax.axis_size("dp"), lax.axis_size("fsdp")
    vectors = [
        query_bias_vector, value_bias_vector, out_bias, gain_one, shift_one, down_bias, gain_two, shift_two
    ]
    order = shard_order(dp, fsdp)
    first = along_z(pack(qkv_weight, vectors, up_bias), dp, fsdp)
    second = along_z(after(jnp.concatenate([out_weight, up_weight], axis=1), first), dp, fsdp)
    third = along_z(after(down_weight, second), dp, fsdp)
    output, terms, rest = compute(
        order, inputs, segment_ids, cotangent,
        spread(first, dp, fsdp), spread(second, dp, fsdp), spread(third, dp, fsdp),
        (query_down, query_up_weight, value_down, value_up_weight),
    )
    terms = sum_everywhere(terms, dp, fsdp)
    rank = query_down.shape[1]
    return (
        output, rest(),
        terms[:rank].T, terms[rank : 2 * rank], terms[2 * rank : 3 * rank].T, terms[3 * rank :],
    )


def solution(mesh):
    split = AXES
    in_specs = (
        (P(split, None, None), P(split, None), P(split, None, None))
        + (P(split, None),) * 4
        + (P(split),) * 9
        + (P(),) * 4
    )
    out_specs = (P(split, None, None), P(split, None, None), P(), P(), P(), P())
    return jax.shard_map(local, mesh=mesh, in_specs=in_specs, out_specs=out_specs, check_vma=False)
```
